32 devices in a mesh: gx: 16 (over z, x, core), yz: 2 (over y).
Axes of the slice: x: 2, y: 2, z: 4, core: 2. Of those that a mesh axis runs over, the one named last changes fastest.
Arguments:
- fields: float32 [5, 256, 512], P(None, 'gx', 'yz'), may hold values from 0.03 to 25, as said below
- node_cell: int32 [256, 512], P('gx', 'yz'), may hold values from 0 to 255, as said below
- node_frac: float32 [256, 512], P('gx', 'yz'), as said below
Outputs:
- remapped: float32 [5, 256, 512], P(None, 'gx', 'yz')
- field_mean: float32 [5], replicated
The draws below stay inside these ranges and needn't reach their ends.
Inputs may be any that keep to these rules, and one draw needn't show every extreme that they name: `fields`: fields are positive cell means. For new node k of a pencil, node_cell lies cyclically between k - 14 and k + 13, and both ends are reached in every pencil; consecutive new nodes are at least 0.45 cells apart. `node_frac`: A multiple of 1/1024, below 1.
All inputs are finite; a program needn't handle non-finite values.
Results may differ from the reference program's by a relative error of at most 0.0003.
Values sent between devices are 32-bit elements; how exact they have to be, the bound alone decides.
A program may use at most 64 MiB of HBM per device.

```python
import jax
import jax.numpy as jnp
from jax import lax

F = 5
DISP = 14
NX = 256
NP = 512


frac_levels = 1024


def node_positions(key):
    base_key = jax.random.fold_in(key, 7)
    key_shift, key_jitter = jax.random.split(base_key)
    phase_shift = jax.random.randint(key_shift, (1, NP), 0, NX)
    jitter = jax.random.randint(key_jitter, (NX, NP), -(frac_levels * 15) // 100, frac_levels * 15 // 100 + 1)
    node_index = jnp.arange(NX, dtype=jnp.int32)[:, None]
    phase = (node_index + phase_shift) % NX
    triangle = jnp.where(phase < NX // 2, 4 * phase - NX, 3 * NX - 4 * phase)
    amplitude = DISP * frac_levels - frac_levels * 3 // 10
    offset_units = amplitude * triangle // NX
    position = node_index * frac_levels + offset_units + jitter
    owner_cell = position // frac_levels % NX
    fraction_units = position % frac_levels
    return (owner_cell, fraction_units)


def draw_node_cell(key, part):
    owner_cell, fraction_units = node_positions(key)
    return owner_cell.astype(jnp.int32)


def draw_node_frac(key, part):
    owner_cell, fraction_units = node_positions(key)
    return fraction_units.astype(jnp.float32) / frac_levels


def draw_fields(key, part):
    key_scale, key_rough = jax.random.split(jax.random.fold_in(key, 11), 2)
    along_x = jnp.arange(NX, dtype=jnp.float32) / NX
    along_pencil = jnp.arange(NP, dtype=jnp.float32) / NP
    trend = (1.0 + 2.0 * along_x)[:, None] * (1.0 + 2.0 * along_pencil)[None, :] / 3.0
    field_scale = jnp.exp(jax.random.uniform(key_scale, (F, 1, 1), jnp.float32, jnp.log(0.5), jnp.log(2.0)))
    roughness = jnp.exp(jax.random.uniform(key_rough, (F, NX, NP), jnp.float32, jnp.log(0.5), jnp.log(2.0)))
    values = field_scale * trend[None] * roughness
    return values.astype(jnp.float32)


def setup_inputs(seed: int = 0) -> dict:
    streams_of = jax.random.split(jax.random.key(seed), 4)
    fields = draw_fields(jax.random.fold_in(streams_of[3], 71), 0)
    node_cell = draw_node_cell(jax.random.fold_in(streams_of[3], 71), 0)
    node_frac = draw_node_frac(jax.random.fold_in(streams_of[3], 71), 0)
    return {"fields": fields, "node_cell": node_cell, "node_frac": node_frac}


def legendre_moments(padded):
    interior = padded.shape[-2] - 4
    left_cell = padded[..., 1:interior + 2, :]
    right_cell = padded[..., 2:interior + 3, :]
    faces = (7.0 / 12.0) * (left_cell + right_cell) - (1.0 / 12.0) * (padded[..., 0:interior + 1, :] + padded[..., 3:interior + 4, :])
    faces = jnp.clip(faces, jnp.minimum(left_cell, right_cell), jnp.maximum(left_cell, right_cell))
    means = padded[..., 2:interior + 2, :]
    face_low = faces[..., :interior, :]
    face_high = faces[..., 1:, :]
    is_flat = (face_high - means) * (means - face_low) <= 0.0
    face_low = jnp.where(is_flat, means, face_low)
    face_high = jnp.where(is_flat, means, face_high)
    jump_size = face_high - face_low
    centre = means - 0.5 * (face_low + face_high)
    threshold = jump_size * jump_size / 6.0
    low_final = jnp.where(jump_size * centre > threshold, 3.0 * means - 2.0 * face_high, face_low)
    high_final = jnp.where(-threshold > jump_size * centre, 3.0 * means - 2.0 * face_low, face_high)
    slopes = 0.5 * (high_final - low_final)
    curves = 0.5 * (low_final + high_final) - means
    return slopes, curves


def partial_mass(means, slopes, curves, fraction):
    return fraction * (means + slopes * (fraction - 1.0) + curves * ((2.0 * fraction - 3.0) * fraction + 1.0))


def reference(fields, node_cell, node_frac):
    node_index = jnp.arange(NX, dtype=jnp.int32)[:, None]
    winding = (node_index - node_cell + NX // 2) // NX
    next_cell = jnp.concatenate([node_cell[1:], node_cell[:1]], axis=0)
    next_winding = jnp.concatenate([winding[1:], winding[:1] + 1], axis=0)
    next_frac = jnp.concatenate([node_frac[1:], node_frac[:1]], axis=0)
    widths = ((next_cell + next_winding * NX) - (node_cell + winding * NX)).astype(node_frac.dtype) + next_frac - node_frac

    def one_field(column):
        padded = jnp.concatenate([column[-2:], column, column[:2]], axis=0)
        slopes, curves = legendre_moments(padded)
        loop_mass = jnp.sum(column, axis=0)
        mass_before = jnp.cumsum(column, axis=0) - column

        def select_rows(values):
            return jnp.take_along_axis(values, node_cell, axis=0)

        mass_at = select_rows(mass_before) + partial_mass(select_rows(column), select_rows(slopes), select_rows(curves), node_frac)
        mass_at = mass_at + winding.astype(column.dtype) * loop_mass[None, :]
        mass_after = jnp.concatenate([mass_at[1:], mass_at[:1] + loop_mass[None, :]], axis=0)
        masses = mass_after - mass_at
        return masses / widths, jnp.sum(masses)

    remapped, field_sums = lax.map(one_field, fields)
    field_mean = field_sums / (NX * NP)
    return remapped, field_mean
```

```python
import functools

import jax
import jax.numpy as jnp
from jax import lax
from jax.experimental import pallas as pl
from jax.experimental.pallas import tpu as pltpu
from jax.sharding import PartitionSpec as P

MESH = pl.DeviceIdType.MESH
LANES = 128
SUB = 8


def legendre_moments(means):
    rows = means.shape[0]
    right = pltpu.roll(means, rows - 1, 0)
    outer = pltpu.roll(means, 1, 0) + pltpu.roll(means, rows - 2, 0)
    faces = 7.0 / 12.0 * (means + right) - 1.0 / 12.0 * outer
    faces = jnp.clip(faces, jnp.minimum(means, right), jnp.maximum(means, right))
    face_low = pltpu.roll(faces, 1, 0)
    face_high = faces
    is_flat = (face_high - means) * (means - face_low) <= 0.0
    face_low = jnp.where(is_flat, means, face_low)
    face_high = jnp.where(is_flat, means, face_high)
    jump_size = face_high - face_low
    centre = means - 0.5 * (face_low + face_high)
    threshold = jump_size * jump_size * (1.0 / 6.0)
    tilt = jump_size * centre
    low_final = jnp.where(tilt > threshold, 3.0 * means - 2.0 * face_high, face_low)
    high_final = jnp.where(-threshold > tilt, 3.0 * means - 2.0 * face_low, face_high)
    slopes = 0.5 * (high_final - low_final)
    curves = 0.5 * (low_final + high_final) - means
    return slopes, curves


def pick(table, index):
    return jnp.take_along_axis(table, index, axis=0, mode="promise_in_bounds")


def kernel(
    sizes, fields_ref, cell_ref, frac_ref, out_ref, mean_ref,
    ext, nodes, fracs, slots, local_sem, send_sem, recv_sem, msg_send, msg_recv,
):
    segments, slabs, field_count, cells, pencils = sizes
    total = segments * slabs
    length = segments * cells
    margin = cells - 2
    own = lax.axis_index("gx")
    slab = lax.axis_index("yz")
    me = own * slabs + slab
    root = own * cells

    def peer(step):
        flat = lax.rem(me + step, total)
        return {"gx": flat // slabs, "yz": lax.rem(flat, slabs)}

    load_fields = pltpu.make_async_copy(fields_ref, ext.at[:, pl.ds(cells, cells)], local_sem.at[0])
    load_cell = pltpu.make_async_copy(cell_ref, nodes.at[pl.ds(0, cells)], local_sem.at[1])
    load_frac = pltpu.make_async_copy(frac_ref, fracs.at[pl.ds(0, cells)], local_sem.at[2])
    load_fields.start()
    load_cell.start()
    load_frac.start()

    barrier = pltpu.get_barrier_semaphore()

    def greet(step, carry):
        pl.semaphore_signal(barrier, inc=1, device_id=peer(step), device_id_type=MESH)
        return carry

    lax.fori_loop(1, total, greet, 0)

    load_fields.wait()
    lane = lax.broadcasted_iota(jnp.int32, (1, LANES), 1)
    message = jnp.zeros((1, LANES), jnp.float32)
    for f in range(field_count):
        part = jnp.sum(ext[f, cells : 2 * cells, :], keepdims=True)
        message = jnp.where(lane == f, part, message)
    slots[0] = message
    load_cell.wait()
    load_frac.wait()
    pl.semaphore_wait(barrier, total - 1)

    right = {"gx": lax.rem(own + 1, segments)}
    left = {"gx": lax.rem(own + segments - 1, segments)}
    block = ext.at[:, pl.ds(cells, cells)]
    copies = [
        (nodes.at[pl.ds(0, SUB)], nodes.at[pl.ds(cells, SUB)], left),
        (fracs.at[pl.ds(0, SUB)], fracs.at[pl.ds(cells, SUB)], left),
        (block, ext.at[:, pl.ds(2 * cells, cells)], left),
        (block, ext.at[:, pl.ds(0, cells)], right),
    ]
    copies = [
        pltpu.make_async_remote_copy(
            src_ref=source, dst_ref=target, send_sem=send_sem.at[i], recv_sem=recv_sem.at[i],
            device_id=who, device_id_type=MESH,
        )
        for i, (source, target, who) in enumerate(copies)
    ]
    for copy in copies:
        copy.start()

    def send(step, carry):
        pltpu.make_async_remote_copy(
            src_ref=slots.at[0], dst_ref=slots.at[step], send_sem=msg_send, recv_sem=msg_recv,
            device_id=peer(step), device_id_type=MESH,
        ).start()
        return carry

    lax.fori_loop(1, total, send, 0)
    for copy in copies:
        copy.wait_recv()

    node_rows = cells + SUB
    node_index = root + lax.broadcasted_iota(jnp.int32, (node_rows, LANES), 0)
    row_id = lax.broadcasted_iota(jnp.int32, (cells, LANES), 0)
    groups = 3 * cells // SUB
    origin = cells // SUB
    low_row = cells - margin
    high_row = cells + margin - 1
    sub_id = lax.broadcasted_iota(jnp.int32, (groups, SUB, LANES), 1)

    for half in range(pencils // LANES):
        span = slice(half * LANES, (half + 1) * LANES)
        cell = nodes[:, span]
        frac = fracs[:, span]
        shifted = node_index - cell + length // 2
        cell = jnp.where(shifted < 0, cell - length, jnp.where(shifted >= length, cell + length, cell))
        place = cell - root + cells
        group = place // SUB
        index = place % SUB
        position = place.astype(jnp.float32)
        after_cell = jnp.concatenate([position[1:cells], position[cells : cells + 1]], axis=0)
        after_frac = jnp.concatenate([frac[1:cells], frac[cells : cells + 1]], axis=0)
        inverse = 1.0 / ((after_cell - position[:cells]) + after_frac - frac[:cells])

        for f in range(field_count):
            means = ext[f, :, span]
            slopes, curves = legendre_moments(means)
            stack = means.reshape(groups, SUB, LANES)
            running = stack
            for step in (1, 2, 4):
                running = running + jnp.where(sub_id >= step, pltpu.roll(running, step, 1), 0.0)
            before = running - stack
            bases = [None] * groups
            bases[origin] = jnp.zeros((1, LANES), jnp.float32)
            for g in range(origin + 1, groups):
                bases[g] = bases[g - 1] + running[g - 1, SUB - 1 : SUB]
            for g in range(origin - 1, -1, -1):
                bases[g] = bases[g + 1] - running[g, SUB - 1 : SUB]
            tables = []
            for g in range(groups):
                at = slice(g * SUB, (g + 1) * SUB)
                tables.append((before[g] + bases[g], stack[g], slopes[at], curves[at]))

            blocks = []
            for b in range(cells // SUB + 1):
                at = slice(b * SUB, (b + 1) * SUB)
                first = (b * SUB + low_row) // SUB
                last_node = b * SUB + SUB - 1 if b < cells // SUB else b * SUB
                last = (last_node + high_row) // SUB
                chosen = [None] * 4
                for g in range(first, last + 1):
                    for i in range(4):
                        got = pick(tables[g][i], index[at])
                        chosen[i] = got if chosen[i] is None else jnp.where(group[at] == g, got, chosen[i])
                t = frac[at]
                base, mean, slope, curve = chosen
                blocks.append(
                    base + t * (mean + slope * (t - 1.0) + curve * ((2.0 * t - 3.0) * t + 1.0))
                )
            mass = jnp.concatenate(blocks[:-1], axis=0)
            after = jnp.where(row_id == cells - 1, blocks[-1][0:1], pltpu.roll(mass, cells - 1, 0))
            out_ref[f, :, span] = (after - mass) * inverse

    arrived = pltpu.make_async_copy(
        slots.at[pl.ds(1, total - 1)], slots.at[pl.ds(1, total - 1)], msg_recv
    )
    arrived.wait()
    summed = jnp.sum(slots[...], axis=0) * (1.0 / (length * pencils * slabs))
    mean_ref[...] = summed
    for copy in copies:
        copy.wait_send()
    pltpu.make_async_copy(
        slots.at[pl.ds(1, total - 1)], slots.at[pl.ds(1, total - 1)], msg_send
    ).wait()


def shards(fields, node_cell, node_frac):
    field_count, cells, pencils = fields.shape
    segments = lax.axis_size("gx")
    slabs = lax.axis_size("yz")
    total = segments * slabs
    sizes = (segments, slabs, field_count, cells, pencils)
    dma = pltpu.SemaphoreType.DMA
    remapped, mean = pl.pallas_call(
        functools.partial(kernel, sizes),
        out_shape=(
            jax.ShapeDtypeStruct(fields.shape, jnp.float32),
            jax.ShapeDtypeStruct((1, LANES), jnp.float32),
        ),
        in_specs=[pl.BlockSpec(memory_space=pl.ANY)] * 3,
        out_specs=(
            pl.BlockSpec(memory_space=pltpu.VMEM),
            pl.BlockSpec(memory_space=pltpu.VMEM),
        ),
        scratch_shapes=[
            pltpu.VMEM((field_count, 3 * cells, pencils), jnp.float32),
            pltpu.VMEM((cells + SUB, pencils), jnp.int32),
            pltpu.VMEM((cells + SUB, pencils), jnp.float32),
            pltpu.VMEM((total, 1, LANES), jnp.float32),
            dma((3,)),
            dma((4,)),
            dma((4,)),
            dma,
            dma,
        ],
        compiler_params=pltpu.CompilerParams(collective_id=0, has_side_effects=True),
    )(fields, node_cell, node_frac)
    return remapped, mean[0, :field_count]


def solution(mesh):
    in_specs = (P(None, "gx", "yz"), P("gx", "yz"), P("gx", "yz"))
    out_specs = (P(None, "gx", "yz"), P())
    return jax.shard_map(shards, mesh=mesh, in_specs=in_specs, out_specs=out_specs, check_vma=False)
```

```python
import functools

import jax
import jax.numpy as jnp
from jax import lax
from jax.experimental import pallas as pl
from jax.experimental.pallas import tpu as pltpu
from jax.sharding import PartitionSpec as P

MESH = pl.DeviceIdType.MESH
LANES = 128
SUB = 8


def legendre_moments(means):
    rows = means.shape[0]
    right = pltpu.roll(means, rows - 1, 0)
    outer = pltpu.roll(means, 1, 0) + pltpu.roll(means, rows - 2, 0)
    faces = 7.0 / 12.0 * (means + right) - 1.0 / 12.0 * outer
    faces = jnp.clip(faces, jnp.minimum(means, right), jnp.maximum(means, right))
    face_low = pltpu.roll(faces, 1, 0)
    face_high = faces
    is_flat = (face_high - means) * (means - face_low) <= 0.0
    face_low = jnp.where(is_flat, means, face_low)
    face_high = jnp.where(is_flat, means, face_high)
    jump_size = face_high - face_low
    centre = means - 0.5 * (face_low + face_high)
    threshold = jump_size * jump_size * (1.0 / 6.0)
    tilt = jump_size * centre
    low_final = jnp.where(tilt > threshold, 3.0 * means - 2.0 * face_high, face_low)
    high_final = jnp.where(-threshold > tilt, 3.0 * means - 2.0 * face_low, face_high)
    slopes = 0.5 * (high_final - low_final)
    curves = 0.5 * (low_final + high_final) - means
    return slopes, curves


def pick(table, index):
    return jnp.take_along_axis(table, index, axis=0, mode="promise_in_bounds")


def kernel(
    sizes, fields_ref, cell_ref, frac_ref, out_ref, mean_ref,
    ext, nodes, fracs, slots, local_sem, send_sem, recv_sem, msg_send, msg_recv,
):
    segments, slabs, field_count, cells, pencils = sizes
    total = segments * slabs
    length = segments * cells
    margin = cells - 2
    own = lax.axis_index("gx")
    slab = lax.axis_index("yz")
    me = own * slabs + slab
    root = own * cells

    def peer(step):
        flat = lax.rem(me + step, total)
        return {"gx": flat // slabs, "yz": lax.rem(flat, slabs)}

    load_fields = pltpu.make_async_copy(fields_ref, ext.at[:, pl.ds(cells, cells)], local_sem.at[0])
    load_cell = pltpu.make_async_copy(cell_ref, nodes.at[pl.ds(0, cells)], local_sem.at[1])
    load_frac = pltpu.make_async_copy(frac_ref, fracs.at[pl.ds(0, cells)], local_sem.at[2])
    load_fields.start()
    load_cell.start()
    load_frac.start()

    barrier = pltpu.get_barrier_semaphore()

    def greet(step, carry):
        pl.semaphore_signal(barrier, inc=1, device_id=peer(step), device_id_type=MESH)
        return carry

    lax.fori_loop(1, total, greet, 0)

    load_fields.wait()
    lane = lax.broadcasted_iota(jnp.int32, (1, LANES), 1)
    message = jnp.zeros((1, LANES), jnp.float32)
    for f in range(field_count):
        part = jnp.sum(ext[f, cells : 2 * cells, :], keepdims=True)
        message = jnp.where(lane == f, part, message)
    slots[0] = message
    load_cell.wait()
    load_frac.wait()
    pl.semaphore_wait(barrier, total - 1)

    right = {"gx": lax.rem(own + 1, segments)}
    left = {"gx": lax.rem(own + segments - 1, segments)}
    block = ext.at[:, pl.ds(cells, cells)]
    copies = [
        (nodes.at[pl.ds(0, SUB)], nodes.at[pl.ds(cells, SUB)], left),
        (fracs.at[pl.ds(0, SUB)], fracs.at[pl.ds(cells, SUB)], left),
        (block, ext.at[:, pl.ds(2 * cells, cells)], left),
        (block, ext.at[:, pl.ds(0, cells)], right),
    ]
    copies = [
        pltpu.make_async_remote_copy(
            src_ref=source, dst_ref=target, send_sem=send_sem.at[i], recv_sem=recv_sem.at[i],
            device_id=who, device_id_type=MESH,
        )
        for i, (source, target, who) in enumerate(copies)
    ]
    for copy in copies:
        copy.start()

    def send(step, carry):
        pltpu.make_async_remote_copy(
            src_ref=slots.at[0], dst_ref=slots.at[step], send_sem=msg_send, recv_sem=msg_recv,
            device_id=peer(step), device_id_type=MESH,
        ).start()
        return carry

    lax.fori_loop(1, total, send, 0)
    for copy in copies:
        copy.wait_recv()

    node_rows = cells + SUB
    node_index = root + lax.broadcasted_iota(jnp.int32, (node_rows, LANES), 0)
    row_id = lax.broadcasted_iota(jnp.int32, (cells, LANES), 0)
    groups = 3 * cells // SUB
    origin = cells // SUB
    low_row = cells - margin
    high_row = cells + margin - 1
    sub_id = lax.broadcasted_iota(jnp.int32, (groups, SUB, LANES), 1)

    for half in range(pencils // LANES):
        span = slice(half * LANES, (half + 1) * LANES)
        cell = nodes[:, span]
        frac = fracs[:, span]
        shifted = node_index - cell + length // 2
        cell = jnp.where(shifted < 0, cell - length, jnp.where(shifted >= length, cell + length, cell))
        place = cell - root + cells
        group = place // SUB
        index = place % SUB
        position = place.astype(jnp.float32)
        after_cell = jnp.concatenate([position[1:cells], position[cells : cells + 1]], axis=0)
        after_frac = jnp.concatenate([frac[1:cells], frac[cells : cells + 1]], axis=0)
        inverse = 1.0 / ((after_cell - position[:cells]) + after_frac - frac[:cells])

        for f in range(field_count):
            means = ext[f, :, span]
            slopes, curves = legendre_moments(means)
            stack = means.reshape(groups, SUB, LANES)
            running = stack
            for step in (1, 2, 4):
                running = running + jnp.where(sub_id >= step, pltpu.roll(running, step, 1), 0.0)
            before = running - stack
            bases = [None] * groups
            bases[origin] = jnp.zeros((1, LANES), jnp.float32)
            for g in range(origin + 1, groups):
                bases[g] = bases[g - 1] + running[g - 1, SUB - 1 : SUB]
            for g in range(origin - 1, -1, -1):
                bases[g] = bases[g + 1] - running[g, SUB - 1 : SUB]
            tables = []
            for g in range(groups):
                at = slice(g * SUB, (g + 1) * SUB)
                tables.append((before[g] + bases[g], stack[g], slopes[at], curves[at]))

            blocks = []
            for b in range(cells // SUB + 1):
                at = slice(b * SUB, (b + 1) * SUB)
                first = (b * SUB + low_row) // SUB
                last_node = b * SUB + SUB - 1 if b < cells // SUB else b * SUB
                last = (last_node + high_row) // SUB
                chosen = [None] * 4
                for g in range(first, last + 1):
                    for i in range(4):
                        got = pick(tables[g][i], index[at])
                        chosen[i] = got if chosen[i] is None else jnp.where(group[at] == g, got, chosen[i])
                t = frac[at]
                base, mean, slope, curve = chosen
                blocks.append(
                    base + t * (mean + slope * (t - 1.0) + curve * ((2.0 * t - 3.0) * t + 1.0))
                )
            mass = jnp.concatenate(blocks[:-1], axis=0)
            after = jnp.where(row_id == cells - 1, blocks[-1][0:1], pltpu.roll(mass, cells - 1, 0))
            out_ref[f, :, span] = (after - mass) * inverse

    arrived = pltpu.make_async_copy(
        slots.at[pl.ds(1, total - 1)], slots.at[pl.ds(1, total - 1)], msg_recv
    )
    arrived.wait()
    summed = jnp.sum(slots[...], axis=0) * (1.0 / (length * pencils * slabs))
    mean_ref[...] = summed[0, :field_count]
    for copy in copies:
        copy.wait_send()
    pltpu.make_async_copy(
        slots.at[pl.ds(1, total - 1)], slots.at[pl.ds(1, total - 1)], msg_send
    ).wait()


def put(new_ref, mean_ref, new_out, mean_out, sem):
    new_copy = pltpu.make_async_copy(new_ref, new_out, sem.at[0])
    mean_copy = pltpu.make_async_copy(mean_ref, mean_out, sem.at[1])
    new_copy.start()
    mean_copy.start()
    new_copy.wait()
    mean_copy.wait()


def shards(fields, node_cell, node_frac):
    field_count, cells, pencils = fields.shape
    segments = lax.axis_size("gx")
    slabs = lax.axis_size("yz")
    total = segments * slabs
    sizes = (segments, slabs, field_count, cells, pencils)
    dma = pltpu.SemaphoreType.DMA
    remapped, mean = pl.pallas_call(
        functools.partial(kernel, sizes),
        out_shape=(
            pltpu.VMEM(fields.shape, jnp.float32),
            pltpu.VMEM((field_count,), jnp.float32),
        ),
        in_specs=[pl.BlockSpec(memory_space=pl.ANY)] * 3,
        out_specs=(
            pl.BlockSpec(memory_space=pltpu.VMEM),
            pl.BlockSpec(memory_space=pltpu.VMEM),
        ),
        scratch_shapes=[
            pltpu.VMEM((field_count, 3 * cells, pencils), jnp.float32),
            pltpu.VMEM((cells + SUB, pencils), jnp.int32),
            pltpu.VMEM((cells + SUB, pencils), jnp.float32),
            pltpu.VMEM((total, 1, LANES), jnp.float32),
            dma((3,)),
            dma((4,)),
            dma((4,)),
            dma,
            dma,
        ],
        compiler_params=pltpu.CompilerParams(collective_id=0, has_side_effects=True),
    )(fields, node_cell, node_frac)
    return pl.pallas_call(
        put,
        out_shape=(
            jax.ShapeDtypeStruct(fields.shape, jnp.float32),
            jax.ShapeDtypeStruct((field_count,), jnp.float32),
        ),
        in_specs=[pl.BlockSpec(memory_space=pltpu.VMEM)] * 2,
        out_specs=(pl.BlockSpec(memory_space=pl.ANY),) * 2,
        scratch_shapes=[dma((2,))],
    )(
        pltpu.with_memory_space_constraint(remapped, pltpu.VMEM),
        pltpu.with_memory_space_constraint(mean, pltpu.VMEM),
    )


def solution(mesh):
    in_specs = (P(None, "gx", "yz"), P("gx", "yz"), P("gx", "yz"))
    out_specs = (P(None, "gx", "yz"), P())
    return jax.shard_map(shards, mesh=mesh, in_specs=in_specs, out_specs=out_specs, check_vma=False)
```

```python
import functools

import jax
import jax.numpy as jnp
from jax import lax
from jax.experimental import pallas as pl
from jax.experimental.pallas import tpu as pltpu
from jax.sharding import PartitionSpec as P

MESH = pl.DeviceIdType.MESH
LANES = 128
SUB = 8


def legendre_moments(means):
    rows = means.shape[0]
    right = pltpu.roll(means, rows - 1, 0)
    outer = pltpu.roll(means, 1, 0) + pltpu.roll(means, rows - 2, 0)
    faces = 7.0 / 12.0 * (means + right) - 1.0 / 12.0 * outer
    faces = jnp.clip(faces, jnp.minimum(means, right), jnp.maximum(means, right))
    face_low = pltpu.roll(faces, 1, 0)
    face_high = faces
    is_flat = (face_high - means) * (means - face_low) <= 0.0
    face_low = jnp.where(is_flat, means, face_low)
    face_high = jnp.where(is_flat, means, face_high)
    jump_size = face_high - face_low
    centre = means - 0.5 * (face_low + face_high)
    threshold = jump_size * jump_size * (1.0 / 6.0)
    tilt = jump_size * centre
    low_final = jnp.where(tilt > threshold, 3.0 * means - 2.0 * face_high, face_low)
    high_final = jnp.where(-threshold > tilt, 3.0 * means - 2.0 * face_low, face_high)
    slopes = 0.5 * (high_final - low_final)
    curves = 0.5 * (low_final + high_final) - means
    return slopes, curves


def pick(table, index):
    return jnp.take_along_axis(table, index, axis=0, mode="promise_in_bounds")


def kernel(
    sizes, fields_ref, cell_ref, frac_ref, out_ref, mean_ref,
    ext, nodes, fracs, slots, far_slots, local_sem, send_sem, recv_sem, msg_send, msg_recv,
):
    segments, slabs, blocks, field_count, cells, pencils = sizes
    length = segments * cells
    margin = cells - 2
    own = lax.axis_index("gx")
    slab = lax.axis_index("yz")
    root = own * cells

    width = segments // blocks
    near = width * slabs
    here = lax.rem(own, width) * slabs + slab
    block_id = own // width

    def near_peer(step):
        flat = lax.rem(here + step, near)
        return {"gx": block_id * width + flat // slabs, "yz": lax.rem(flat, slabs)}

    def far_peer(step):
        return {"gx": lax.rem(block_id + step, blocks) * width + lax.rem(own, width)}

    right = {"gx": lax.rem(own + 1, segments)}
    left = {"gx": lax.rem(own + segments - 1, segments)}

    load_fields = pltpu.make_async_copy(fields_ref, ext.at[:, pl.ds(cells, cells)], local_sem.at[0])
    load_cell = pltpu.make_async_copy(cell_ref, nodes.at[pl.ds(0, cells)], local_sem.at[1])
    load_frac = pltpu.make_async_copy(frac_ref, fracs.at[pl.ds(0, cells)], local_sem.at[2])
    load_fields.start()
    load_cell.start()
    load_frac.start()

    barrier = pltpu.get_barrier_semaphore()

    def greet(who):
        pl.semaphore_signal(barrier, inc=1, device_id=who, device_id_type=MESH)

    greet(right)
    greet(left)
    for step in range(1, blocks):
        greet(far_peer(step))

    @pl.loop(1, near)
    def _(step):
        greet(near_peer(step))

    load_fields.wait()
    lane = lax.broadcasted_iota(jnp.int32, (1, LANES), 1)
    message = jnp.zeros((1, LANES), jnp.float32)
    for f in range(field_count):
        part = jnp.sum(ext[f, cells : 2 * cells, :], keepdims=True)
        message = jnp.where(lane == f, part, message)
    slots[0] = message
    load_cell.wait()
    load_frac.wait()
    pl.semaphore_wait(barrier, near + blocks)

    block = ext.at[:, pl.ds(cells, cells)]

    def push(i, source, target, who):
        return pltpu.make_async_remote_copy(
            src_ref=source, dst_ref=target, send_sem=send_sem.at[i], recv_sem=recv_sem.at[i],
            device_id=who, device_id_type=MESH,
        )

    to_left = push(0, block, ext.at[:, pl.ds(2 * cells, cells)], left)
    to_right = push(1, block, ext.at[:, pl.ds(0, cells)], right)
    first_cell = push(2, nodes.at[pl.ds(0, SUB)], nodes.at[pl.ds(cells, SUB)], left)
    first_frac = push(3, fracs.at[pl.ds(0, SUB)], fracs.at[pl.ds(cells, SUB)], left)
    copies = [to_left, to_right, first_cell, first_frac]

    yield_right = own == 1
    yield_left = own == segments - 2

    @pl.when(jnp.logical_not(yield_right))
    def _():
        to_right.start()

    @pl.when(jnp.logical_not(yield_left))
    def _():
        to_left.start()

    @pl.loop(1, near)
    def _(step):
        pltpu.make_async_remote_copy(
            src_ref=slots.at[0], dst_ref=slots.at[step], send_sem=msg_send.at[0],
            recv_sem=msg_recv.at[0], device_id=near_peer(step), device_id_type=MESH,
        ).start()

    first_cell.start()
    first_frac.start()

    @pl.when(yield_right)
    def _():
        to_right.wait_recv()
        to_right.start()

    @pl.when(yield_left)
    def _():
        to_left.wait_recv()
        to_left.start()

    def all_slots(ref, count, sem):
        part = ref.at[pl.ds(1, count - 1)]
        return pltpu.make_async_copy(part, part, sem)

    all_slots(slots, near, msg_recv.at[0]).wait()
    far_slots[0] = jnp.sum(slots[...], axis=0)
    far_copies = [
        pltpu.make_async_remote_copy(
            src_ref=far_slots.at[0], dst_ref=far_slots.at[step], send_sem=msg_send.at[1],
            recv_sem=msg_recv.at[1], device_id=far_peer(step), device_id_type=MESH,
        )
        for step in range(1, blocks)
    ]
    for copy in far_copies:
        copy.start()

    first_cell.wait_recv()
    first_frac.wait_recv()

    @pl.when(jnp.logical_not(yield_right))
    def _():
        to_right.wait_recv()

    @pl.when(jnp.logical_not(yield_left))
    def _():
        to_left.wait_recv()

    node_rows = cells + SUB
    node_index = root + lax.broadcasted_iota(jnp.int32, (node_rows, LANES), 0)
    row_id = lax.broadcasted_iota(jnp.int32, (cells, LANES), 0)
    groups = 3 * cells // SUB
    origin = cells // SUB
    low_row = cells - margin
    high_row = cells + margin - 1
    sub_id = lax.broadcasted_iota(jnp.int32, (groups, SUB, LANES), 1)

    for half in range(pencils // LANES):
        span = slice(half * LANES, (half + 1) * LANES)
        cell = nodes[:, span]
        frac = fracs[:, span]
        shifted = node_index - cell + length // 2
        cell = jnp.where(shifted < 0, cell - length, jnp.where(shifted >= length, cell + length, cell))
        place = cell - root + cells
        group = place // SUB
        index = place % SUB
        position = place.astype(jnp.float32)
        after_cell = jnp.concatenate([position[1:cells], position[cells : cells + 1]], axis=0)
        after_frac = jnp.concatenate([frac[1:cells], frac[cells : cells + 1]], axis=0)
        inverse = 1.0 / ((after_cell - position[:cells]) + after_frac - frac[:cells])

        for f in range(field_count):
            means = ext[f, :, span]
            slopes, curves = legendre_moments(means)
            stack = means.reshape(groups, SUB, LANES)
            running = stack
            for step in (1, 2, 4):
                running = running + jnp.where(sub_id >= step, pltpu.roll(running, step, 1), 0.0)
            before = running - stack
            bases = [None] * groups
            bases[origin] = jnp.zeros((1, LANES), jnp.float32)
            for g in range(origin + 1, groups):
                bases[g] = bases[g - 1] + running[g - 1, SUB - 1 : SUB]
            for g in range(origin - 1, -1, -1):
                bases[g] = bases[g + 1] - running[g, SUB - 1 : SUB]
            tables = []
            for g in range(groups):
                at = slice(g * SUB, (g + 1) * SUB)
                tables.append((before[g] + bases[g], stack[g], slopes[at], curves[at]))

            parts = []
            for b in range(cells // SUB + 1):
                at = slice(b * SUB, (b + 1) * SUB)
                first = (b * SUB + low_row) // SUB
                last_node = b * SUB + SUB - 1 if b < cells // SUB else b * SUB
                last = (last_node + high_row) // SUB
                chosen = [None] * 4
                for g in range(first, last + 1):
                    for i in range(4):
                        got = pick(tables[g][i], index[at])
                        chosen[i] = got if chosen[i] is None else jnp.where(group[at] == g, got, chosen[i])
                t = frac[at]
                base, mean, slope, curve = chosen
                parts.append(
                    base + t * (mean + slope * (t - 1.0) + curve * ((2.0 * t - 3.0) * t + 1.0))
                )
            mass = jnp.concatenate(parts[:-1], axis=0)
            after = jnp.where(row_id == cells - 1, parts[-1][0:1], pltpu.roll(mass, cells - 1, 0))
            out_ref[f, :, span] = (after - mass) * inverse

    all_slots(far_slots, blocks, msg_recv.at[1]).wait()
    summed = jnp.sum(far_slots[...], axis=0) * (1.0 / (length * pencils * slabs))
    mean_ref[...] = summed[0, :field_count]
    for copy in copies:
        copy.wait_send()
    all_slots(slots, near, msg_send.at[0]).wait()
    all_slots(far_slots, blocks, msg_send.at[1]).wait()


def put(new_ref, mean_ref, new_out, mean_out, sem):
    new_copy = pltpu.make_async_copy(new_ref, new_out, sem.at[0])
    mean_copy = pltpu.make_async_copy(mean_ref, mean_out, sem.at[1])
    new_copy.start()
    mean_copy.start()
    new_copy.wait()
    mean_copy.wait()


def shards(fields, node_cell, node_frac):
    field_count, cells, pencils = fields.shape
    segments = lax.axis_size("gx")
    slabs = lax.axis_size("yz")
    blocks = next(n for n in (4, 2) if segments % n == 0)
    sizes = (segments, slabs, blocks, field_count, cells, pencils)
    dma = pltpu.SemaphoreType.DMA
    remapped, mean = pl.pallas_call(
        functools.partial(kernel, sizes),
        out_shape=(
            pltpu.VMEM(fields.shape, jnp.float32),
            pltpu.VMEM((field_count,), jnp.float32),
        ),
        in_specs=[pl.BlockSpec(memory_space=pl.ANY)] * 3,
        out_specs=(
            pl.BlockSpec(memory_space=pltpu.VMEM),
            pl.BlockSpec(memory_space=pltpu.VMEM),
        ),
        scratch_shapes=[
            pltpu.VMEM((field_count, 3 * cells, pencils), jnp.float32),
            pltpu.VMEM((cells + SUB, pencils), jnp.int32),
            pltpu.VMEM((cells + SUB, pencils), jnp.float32),
            pltpu.VMEM((segments // blocks * slabs, 1, LANES), jnp.float32),
            pltpu.VMEM((blocks, 1, LANES), jnp.float32),
            dma((3,)),
            dma((4,)),
            dma((4,)),
            dma((2,)),
            dma((2,)),
        ],
        compiler_params=pltpu.CompilerParams(collective_id=0, has_side_effects=True),
    )(fields, node_cell, node_frac)
    return pl.pallas_call(
        put,
        out_shape=(
            jax.ShapeDtypeStruct(fields.shape, jnp.float32),
            jax.ShapeDtypeStruct((field_count,), jnp.float32),
        ),
        in_specs=[pl.BlockSpec(memory_space=pltpu.VMEM)] * 2,
        out_specs=(pl.BlockSpec(memory_space=pl.ANY),) * 2,
        scratch_shapes=[dma((2,))],
    )(
        pltpu.with_memory_space_constraint(remapped, pltpu.VMEM),
        pltpu.with_memory_space_constraint(mean, pltpu.VMEM),
    )


def solution(mesh):
    in_specs = (P(None, "gx", "yz"), P("gx", "yz"), P("gx", "yz"))
    out_specs = (P(None, "gx", "yz"), P())
    return jax.shard_map(shards, mesh=mesh, in_specs=in_specs, out_specs=out_specs, check_vma=False)
```

```python
import functools

import jax
import jax.numpy as jnp
from jax import lax
from jax.experimental import pallas as pl
from jax.experimental.pallas import tpu as pltpu
from jax.sharding import PartitionSpec as P

MESH = pl.DeviceIdType.MESH
LANES = 128
SUB = 8


def legendre_moments(means):
    rows = means.shape[0]
    right = pltpu.roll(means, rows - 1, 0)
    outer = pltpu.roll(means, 1, 0) + pltpu.roll(means, rows - 2, 0)
    faces = 7.0 / 12.0 * (means + right) - 1.0 / 12.0 * outer
    faces = jnp.clip(faces, jnp.minimum(means, right), jnp.maximum(means, right))
    face_low = pltpu.roll(faces, 1, 0)
    face_high = faces
    is_flat = (face_high - means) * (means - face_low) <= 0.0
    face_low = jnp.where(is_flat, means, face_low)
    face_high = jnp.where(is_flat, means, face_high)
    jump_size = face_high - face_low
    centre = means - 0.5 * (face_low + face_high)
    threshold = jump_size * jump_size * (1.0 / 6.0)
    tilt = jump_size * centre
    low_final = jnp.where(tilt > threshold, 3.0 * means - 2.0 * face_high, face_low)
    high_final = jnp.where(-threshold > tilt, 3.0 * means - 2.0 * face_low, face_high)
    slopes = 0.5 * (high_final - low_final)
    curves = 0.5 * (low_final + high_final) - means
    return slopes, curves


def pick(table, index):
    return jnp.take_along_axis(table, index, axis=0, mode="promise_in_bounds")


def kernel(
    sizes, fields_ref, cell_ref, frac_ref, out_ref, mean_ref,
    ext, nodes, fracs, slots, local_sem, send_sem, recv_sem, msg_send, msg_recv,
):
    segments, slabs, field_count, cells, pencils = sizes
    total = segments * slabs
    length = segments * cells
    margin = cells - 2
    own = lax.axis_index("gx")
    slab = lax.axis_index("yz")
    root = own * cells

    def wrap(value, size):
        return jnp.where(value >= size, value - size, value)

    def others(visit):
        for dy in range(1, slabs):
            visit(dy, {"yz": wrap(slab + dy, slabs)})

        @pl.loop(1, segments)
        def _(dx):
            gx = wrap(own + dx, segments)
            for dy in range(slabs):
                visit(dx * slabs + dy, {"gx": gx, "yz": wrap(slab + dy, slabs)})

    load_fields = pltpu.make_async_copy(fields_ref, ext.at[:, pl.ds(cells, cells)], local_sem.at[0])
    load_cell = pltpu.make_async_copy(cell_ref, nodes.at[pl.ds(0, cells)], local_sem.at[1])
    load_frac = pltpu.make_async_copy(frac_ref, fracs.at[pl.ds(0, cells)], local_sem.at[2])
    load_fields.start()
    load_cell.start()
    load_frac.start()

    barrier = pltpu.get_barrier_semaphore()

    def greet(slot, who):
        pl.semaphore_signal(barrier, inc=1, device_id=who, device_id_type=MESH)

    others(greet)
    load_fields.wait()
    lane = lax.broadcasted_iota(jnp.int32, (1, LANES), 1)
    message = jnp.zeros((1, LANES), jnp.float32)
    for f in range(field_count):
        part = jnp.sum(ext[f, cells : 2 * cells, :], keepdims=True)
        message = jnp.where(lane == f, part, message)
    slots[0] = message
    load_cell.wait()
    load_frac.wait()
    pl.semaphore_wait(barrier, total - 1)

    right = {"gx": wrap(own + 1, segments)}
    left = {"gx": wrap(own + segments - 1, segments)}
    copies = [
        (nodes.at[pl.ds(0, SUB)], nodes.at[pl.ds(cells, SUB)], left),
        (fracs.at[pl.ds(0, SUB)], fracs.at[pl.ds(cells, SUB)], left),
    ]
    for f in range(field_count):
        block = ext.at[f, pl.ds(cells, cells)]
        copies.append((block, ext.at[f, pl.ds(2 * cells, cells)], left))
        copies.append((block, ext.at[f, pl.ds(0, cells)], right))
    copies = [
        pltpu.make_async_remote_copy(
            src_ref=source, dst_ref=target, send_sem=send_sem.at[i], recv_sem=recv_sem.at[i],
            device_id=who, device_id_type=MESH,
        )
        for i, (source, target, who) in enumerate(copies)
    ]
    def send(slot, who):
        pltpu.make_async_remote_copy(
            src_ref=slots.at[0], dst_ref=slots.at[slot], send_sem=msg_send, recv_sem=msg_recv,
            device_id=who, device_id_type=MESH,
        ).start()

    others(send)
    for copy in copies:
        copy.start()
    for copy in copies[:2]:
        copy.wait_recv()

    node_rows = cells + SUB
    node_index = root + lax.broadcasted_iota(jnp.int32, (node_rows, LANES), 0)
    row_id = lax.broadcasted_iota(jnp.int32, (cells, LANES), 0)
    groups = 3 * cells // SUB
    origin = cells // SUB
    low_row = cells - margin
    high_row = cells + margin - 1
    sub_id = lax.broadcasted_iota(jnp.int32, (groups, SUB, LANES), 1)

    halves = []
    for half in range(pencils // LANES):
        span = slice(half * LANES, (half + 1) * LANES)
        cell = nodes[:, span]
        frac = fracs[:, span]
        shifted = node_index - cell + length // 2
        cell = jnp.where(shifted < 0, cell - length, jnp.where(shifted >= length, cell + length, cell))
        place = cell - root + cells
        group = place // SUB
        index = place % SUB
        position = place.astype(jnp.float32)
        after_cell = jnp.concatenate([position[1:cells], position[cells : cells + 1]], axis=0)
        after_frac = jnp.concatenate([frac[1:cells], frac[cells : cells + 1]], axis=0)
        inverse = 1.0 / ((after_cell - position[:cells]) + after_frac - frac[:cells])

        halves.append((span, frac, group, index, inverse))

    for f in range(field_count):
        for copy in copies[2 + 2 * f : 4 + 2 * f]:
            copy.wait_recv()
        for span, frac, group, index, inverse in halves:
            means = ext[f, :, span]
            slopes, curves = legendre_moments(means)
            stack = means.reshape(groups, SUB, LANES)
            running = stack
            for step in (1, 2, 4):
                running = running + jnp.where(sub_id >= step, pltpu.roll(running, step, 1), 0.0)
            before = running - stack
            bases = [None] * groups
            bases[origin] = jnp.zeros((1, LANES), jnp.float32)
            for g in range(origin + 1, groups):
                bases[g] = bases[g - 1] + running[g - 1, SUB - 1 : SUB]
            for g in range(origin - 1, -1, -1):
                bases[g] = bases[g + 1] - running[g, SUB - 1 : SUB]
            tables = []
            for g in range(groups):
                at = slice(g * SUB, (g + 1) * SUB)
                tables.append((before[g] + bases[g], stack[g], slopes[at], curves[at]))

            blocks = []
            for b in range(cells // SUB + 1):
                at = slice(b * SUB, (b + 1) * SUB)
                first = (b * SUB + low_row) // SUB
                last_node = b * SUB + SUB - 1 if b < cells // SUB else b * SUB
                last = (last_node + high_row) // SUB
                chosen = [None] * 4
                for g in range(first, last + 1):
                    for i in range(4):
                        got = pick(tables[g][i], index[at])
                        chosen[i] = got if chosen[i] is None else jnp.where(group[at] == g, got, chosen[i])
                t = frac[at]
                base, mean, slope, curve = chosen
                blocks.append(
                    base + t * (mean + slope * (t - 1.0) + curve * ((2.0 * t - 3.0) * t + 1.0))
                )
            mass = jnp.concatenate(blocks[:-1], axis=0)
            after = jnp.where(row_id == cells - 1, blocks[-1][0:1], pltpu.roll(mass, cells - 1, 0))
            out_ref[f, :, span] = (after - mass) * inverse

    arrived = pltpu.make_async_copy(
        slots.at[pl.ds(1, total - 1)], slots.at[pl.ds(1, total - 1)], msg_recv
    )
    arrived.wait()
    summed = jnp.sum(slots[...], axis=0) * (1.0 / (length * pencils * slabs))
    mean_ref[...] = summed[0, :field_count]
    for copy in copies:
        copy.wait_send()
    pltpu.make_async_copy(
        slots.at[pl.ds(1, total - 1)], slots.at[pl.ds(1, total - 1)], msg_send
    ).wait()


def put(new_ref, mean_ref, new_out, mean_out, sem):
    new_copy = pltpu.make_async_copy(new_ref, new_out, sem.at[0])
    mean_copy = pltpu.make_async_copy(mean_ref, mean_out, sem.at[1])
    new_copy.start()
    mean_copy.start()
    new_copy.wait()
    mean_copy.wait()


def shards(fields, node_cell, node_frac):
    field_count, cells, pencils = fields.shape
    segments = lax.axis_size("gx")
    slabs = lax.axis_size("yz")
    total = segments * slabs
    sizes = (segments, slabs, field_count, cells, pencils)
    dma = pltpu.SemaphoreType.DMA
    remapped, mean = pl.pallas_call(
        functools.partial(kernel, sizes),
        out_shape=(
            pltpu.VMEM(fields.shape, jnp.float32),
            pltpu.VMEM((field_count,), jnp.float32),
        ),
        in_specs=[pl.BlockSpec(memory_space=pl.ANY)] * 3,
        out_specs=(
            pl.BlockSpec(memory_space=pltpu.VMEM),
            pl.BlockSpec(memory_space=pltpu.VMEM),
        ),
        scratch_shapes=[
            pltpu.VMEM((field_count, 3 * cells, pencils), jnp.float32),
            pltpu.VMEM((cells + SUB, pencils), jnp.int32),
            pltpu.VMEM((cells + SUB, pencils), jnp.float32),
            pltpu.VMEM((total, 1, LANES), jnp.float32),
            dma((3,)),
            dma((2 + 2 * field_count,)),
            dma((2 + 2 * field_count,)),
            dma,
            dma,
        ],
        compiler_params=pltpu.CompilerParams(collective_id=0, has_side_effects=True),
    )(fields, node_cell, node_frac)
    return pl.pallas_call(
        put,
        out_shape=(
            jax.ShapeDtypeStruct(fields.shape, jnp.float32),
            jax.ShapeDtypeStruct((field_count,), jnp.float32),
        ),
        in_specs=[pl.BlockSpec(memory_space=pltpu.VMEM)] * 2,
        out_specs=(pl.BlockSpec(memory_space=pl.ANY),) * 2,
        scratch_shapes=[dma((2,))],
    )(
        pltpu.with_memory_space_constraint(remapped, pltpu.VMEM),
        pltpu.with_memory_space_constraint(mean, pltpu.VMEM),
    )


def solution(mesh):
    in_specs = (P(None, "gx", "yz"), P("gx", "yz"), P("gx", "yz"))
    out_specs = (P(None, "gx", "yz"), P())
    return jax.shard_map(shards, mesh=mesh, in_specs=in_specs, out_specs=out_specs, check_vma=False)
```

```python
import functools

import jax
import jax.numpy as jnp
from jax import lax
from jax.experimental import pallas as pl
from jax.experimental.pallas import tpu as pltpu
from jax.sharding import PartitionSpec as P

MESH = pl.DeviceIdType.MESH
LANES = 128
SUB = 8


def legendre_moments(means):
    rows = means.shape[0]
    right = pltpu.roll(means, rows - 1, 0)
    outer = pltpu.roll(means, 1, 0) + pltpu.roll(means, rows - 2, 0)
    faces = 7.0 / 12.0 * (means + right) - 1.0 / 12.0 * outer
    faces = jnp.clip(faces, jnp.minimum(means, right), jnp.maximum(means, right))
    face_low = pltpu.roll(faces, 1, 0)
    face_high = faces
    is_flat = (face_high - means) * (means - face_low) <= 0.0
    face_low = jnp.where(is_flat, means, face_low)
    face_high = jnp.where(is_flat, means, face_high)
    jump_size = face_high - face_low
    centre = means - 0.5 * (face_low + face_high)
    threshold = jump_size * jump_size * (1.0 / 6.0)
    tilt = jump_size * centre
    low_final = jnp.where(tilt > threshold, 3.0 * means - 2.0 * face_high, face_low)
    high_final = jnp.where(-threshold > tilt, 3.0 * means - 2.0 * face_low, face_high)
    slopes = 0.5 * (high_final - low_final)
    curves = 0.5 * (low_final + high_final) - means
    return slopes, curves


def pick(table, index):
    return jnp.take_along_axis(table, index, axis=0, mode="promise_in_bounds")


def kernel(
    sizes, fields_ref, cell_ref, frac_ref, out_ref, mean_ref,
    ext, nodes, fracs, slots, local_sem, send_sem, recv_sem, msg_send, msg_recv,
):
    segments, slabs, field_count, cells, pencils = sizes
    total = segments * slabs
    length = segments * cells
    margin = cells - 2
    own = lax.axis_index("gx")
    slab = lax.axis_index("yz")
    root = own * cells

    def wrap(value, size):
        return jnp.where(value >= size, value - size, value)

    def others(visit):
        for dy in range(1, slabs):
            visit(dy, {"yz": wrap(slab + dy, slabs)})

        @pl.loop(1, segments)
        def _(dx):
            gx = wrap(own + dx, segments)
            for dy in range(slabs):
                visit(dx * slabs + dy, {"gx": gx, "yz": wrap(slab + dy, slabs)})

    load_fields = pltpu.make_async_copy(fields_ref, ext.at[:, pl.ds(cells, cells)], local_sem.at[0])
    load_cell = pltpu.make_async_copy(cell_ref, nodes.at[pl.ds(0, cells)], local_sem.at[1])
    load_frac = pltpu.make_async_copy(frac_ref, fracs.at[pl.ds(0, cells)], local_sem.at[2])
    load_fields.start()
    load_cell.start()
    load_frac.start()

    barrier = pltpu.get_barrier_semaphore()

    def greet(slot, who):
        pl.semaphore_signal(barrier, inc=1, device_id=who, device_id_type=MESH)

    others(greet)
    load_fields.wait()
    lane = lax.broadcasted_iota(jnp.int32, (1, LANES), 1)
    message = jnp.zeros((1, LANES), jnp.float32)
    for f in range(field_count):
        part = jnp.sum(ext[f, cells : 2 * cells, :], keepdims=True)
        message = jnp.where(lane == f, part, message)
    slots[0] = message
    load_cell.wait()
    load_frac.wait()
    pl.semaphore_wait(barrier, total - 1)

    right = {"gx": wrap(own + 1, segments)}
    left = {"gx": wrap(own + segments - 1, segments)}
    copies = [
        (nodes.at[pl.ds(0, SUB)], nodes.at[pl.ds(cells, SUB)], left),
        (fracs.at[pl.ds(0, SUB)], fracs.at[pl.ds(cells, SUB)], left),
    ]
    for f in range(field_count):
        block = ext.at[f, pl.ds(cells, cells)]
        copies.append((block, ext.at[f, pl.ds(2 * cells, cells)], left))
        copies.append((block, ext.at[f, pl.ds(0, cells)], right))
    copies = [
        pltpu.make_async_remote_copy(
            src_ref=source, dst_ref=target, send_sem=send_sem.at[i], recv_sem=recv_sem.at[i],
            device_id=who, device_id_type=MESH,
        )
        for i, (source, target, who) in enumerate(copies)
    ]
    def send(slot, who):
        pltpu.make_async_remote_copy(
            src_ref=slots.at[0], dst_ref=slots.at[slot], send_sem=msg_send, recv_sem=msg_recv,
            device_id=who, device_id_type=MESH,
        ).start()

    for copy in copies[:2]:
        copy.start()
    others(send)
    for copy in copies[2:]:
        copy.start()
    for copy in copies[:2]:
        copy.wait_recv()

    node_rows = cells + SUB
    node_index = root + lax.broadcasted_iota(jnp.int32, (node_rows, LANES), 0)
    row_id = lax.broadcasted_iota(jnp.int32, (cells, LANES), 0)
    groups = 3 * cells // SUB
    origin = cells // SUB
    low_row = cells - margin
    high_row = cells + margin - 1
    sub_id = lax.broadcasted_iota(jnp.int32, (groups, SUB, LANES), 1)

    halves = []
    for half in range(pencils // LANES):
        span = slice(half * LANES, (half + 1) * LANES)
        cell = nodes[:, span]
        frac = fracs[:, span]
        shifted = node_index - cell + length // 2
        cell = jnp.where(shifted < 0, cell - length, jnp.where(shifted >= length, cell + length, cell))
        place = cell - root + cells
        group = place // SUB
        index = place % SUB
        position = place.astype(jnp.float32)
        after_cell = jnp.concatenate([position[1:cells], position[cells : cells + 1]], axis=0)
        after_frac = jnp.concatenate([frac[1:cells], frac[cells : cells + 1]], axis=0)
        inverse = 1.0 / ((after_cell - position[:cells]) + after_frac - frac[:cells])

        halves.append((span, frac, group, index, inverse))

    for f in range(field_count):
        for copy in copies[2 + 2 * f : 4 + 2 * f]:
            copy.wait_recv()
        for span, frac, group, index, inverse in halves:
            means = ext[f, :, span]
            slopes, curves = legendre_moments(means)
            stack = means.reshape(groups, SUB, LANES)
            running = stack
            for step in (1, 2, 4):
                running = running + jnp.where(sub_id >= step, pltpu.roll(running, step, 1), 0.0)
            before = running - stack
            bases = [None] * groups
            bases[origin] = jnp.zeros((1, LANES), jnp.float32)
            for g in range(origin + 1, groups):
                bases[g] = bases[g - 1] + running[g - 1, SUB - 1 : SUB]
            for g in range(origin - 1, -1, -1):
                bases[g] = bases[g + 1] - running[g, SUB - 1 : SUB]
            tables = []
            for g in range(groups):
                at = slice(g * SUB, (g + 1) * SUB)
                tables.append((before[g] + bases[g], stack[g], slopes[at], curves[at]))

            blocks = []
            for b in range(cells // SUB + 1):
                at = slice(b * SUB, (b + 1) * SUB)
                first = (b * SUB + low_row) // SUB
                last_node = b * SUB + SUB - 1 if b < cells // SUB else b * SUB
                last = (last_node + high_row) // SUB
                chosen = [None] * 4
                for g in range(first, last + 1):
                    for i in range(4):
                        got = pick(tables[g][i], index[at])
                        chosen[i] = got if chosen[i] is None else jnp.where(group[at] == g, got, chosen[i])
                t = frac[at]
                base, mean, slope, curve = chosen
                blocks.append(
                    base + t * (mean + slope * (t - 1.0) + curve * ((2.0 * t - 3.0) * t + 1.0))
                )
            mass = jnp.concatenate(blocks[:-1], axis=0)
            after = jnp.where(row_id == cells - 1, blocks[-1][0:1], pltpu.roll(mass, cells - 1, 0))
            out_ref[f, :, span] = (after - mass) * inverse

    arrived = pltpu.make_async_copy(
        slots.at[pl.ds(1, total - 1)], slots.at[pl.ds(1, total - 1)], msg_recv
    )
    arrived.wait()
    summed = jnp.sum(slots[...], axis=0) * (1.0 / (length * pencils * slabs))
    mean_ref[...] = summed[0, :field_count]
    for copy in copies:
        copy.wait_send()
    pltpu.make_async_copy(
        slots.at[pl.ds(1, total - 1)], slots.at[pl.ds(1, total - 1)], msg_send
    ).wait()


def put(new_ref, mean_ref, new_out, mean_out, sem):
    new_copy = pltpu.make_async_copy(new_ref, new_out, sem.at[0])
    mean_copy = pltpu.make_async_copy(mean_ref, mean_out, sem.at[1])
    new_copy.start()
    mean_copy.start()
    new_copy.wait()
    mean_copy.wait()


def shards(fields, node_cell, node_frac):
    field_count, cells, pencils = fields.shape
    segments = lax.axis_size("gx")
    slabs = lax.axis_size("yz")
    total = segments * slabs
    sizes = (segments, slabs, field_count, cells, pencils)
    dma = pltpu.SemaphoreType.DMA
    remapped, mean = pl.pallas_call(
        functools.partial(kernel, sizes),
        out_shape=(
            pltpu.VMEM(fields.shape, jnp.float32),
            pltpu.VMEM((field_count,), jnp.float32),
        ),
        in_specs=[pl.BlockSpec(memory_space=pl.ANY)] * 3,
        out_specs=(
            pl.BlockSpec(memory_space=pltpu.VMEM),
            pl.BlockSpec(memory_space=pltpu.VMEM),
        ),
        scratch_shapes=[
            pltpu.VMEM((field_count, 3 * cells, pencils), jnp.float32),
            pltpu.VMEM((cells + SUB, pencils), jnp.int32),
            pltpu.VMEM((cells + SUB, pencils), jnp.float32),
            pltpu.VMEM((total, 1, LANES), jnp.float32),
            dma((3,)),
            dma((2 + 2 * field_count,)),
            dma((2 + 2 * field_count,)),
            dma,
            dma,
        ],
        compiler_params=pltpu.CompilerParams(collective_id=0, has_side_effects=True),
    )(fields, node_cell, node_frac)
    return pl.pallas_call(
        put,
        out_shape=(
            jax.ShapeDtypeStruct(fields.shape, jnp.float32),
            jax.ShapeDtypeStruct((field_count,), jnp.float32),
        ),
        in_specs=[pl.BlockSpec(memory_space=pltpu.VMEM)] * 2,
        out_specs=(pl.BlockSpec(memory_space=pl.ANY),) * 2,
        scratch_shapes=[dma((2,))],
    )(
        pltpu.with_memory_space_constraint(remapped, pltpu.VMEM),
        pltpu.with_memory_space_constraint(mean, pltpu.VMEM),
    )


def solution(mesh):
    in_specs = (P(None, "gx", "yz"), P("gx", "yz"), P("gx", "yz"))
    out_specs = (P(None, "gx", "yz"), P())
    return jax.shard_map(shards, mesh=mesh, in_specs=in_specs, out_specs=out_specs, check_vma=False)
```
